256 devices in a mesh: ctx: 32 (over x_hi, z, core), head: 8 (over x_lo, y).
Axes of the slice: x: 4 (x_hi: 2, x_lo: 2; x = x_hi * 2 + x_lo), y: 4, z: 8, core: 2. Of those that a mesh axis runs over, the one named last changes fastest.
Arguments:
- queries: bfloat16 [6656, 4096], P('ctx', 'head'), may hold values from -4 to 4
- rotated_key_rows: bfloat16 [6656, 1024], P('ctx', 'head'), may hold values from -4 to 4
- value_matrix: bfloat16 [6656, 1024], P('ctx', 'head'), may hold values from -4 to 4
- out_grad: bfloat16 [6656, 4096], P('ctx', 'head'), may hold values from -6 to 6
- w_out: bfloat16 [4096, 4096], P('head'), may hold values from -0.09375 to 0.09375
- doc_lengths: int32 [16], replicated, may hold values from 1 to 3744, 6656 in all
Outputs:
- grad_q: bfloat16 [6656, 4096], P('ctx', 'head')
- key_gradient: bfloat16 [6656, 1024], P('ctx', 'head')
- value_gradient: bfloat16 [6656, 1024], P('ctx', 'head')
- grad_wo_t: bfloat16 [4096, 4096], P('ctx', 'head')
The draws below stay inside these ranges and needn't reach their ends.
Inputs may be any that keep to these rules, and one draw needn't show every extreme that they name: `doc_lengths`: 16 lengths summing to 6656; the longest is exactly 3744.
All inputs are finite; a program needn't handle non-finite values.
Results may differ from the reference program's by a relative error of at most 0.019.
Values may be sent and summed in bfloat16 or wider, within the bound.
A program may use at most 128 MiB of HBM per device.

```python
import math
import jax
import jax.numpy as jnp
import numpy as np
from jax import lax

D = 4096
QUERY_HEADS = 32
KEY_VALUE_HEADS = 8
HEAD_SIZE = 128
TOK_DEV = 208
DOCS = 16
WINDOW_TOKENS = 6656
MOST = 3744
N_CTX = 32


def with_spikes(result, key, source, target, shards_of, factor):
    owner, partner = [(jnp.arange(result.shape[position]) // (result.shape[position] // shards_of)).reshape([-1 if axis == position else 1 for axis in range(result.ndim)]) for position in (source, target)]
    chosen = jax.random.permutation(key, shards_of)[partner]
    strong = (owner == chosen) | (owner == (partner + shards_of // 2) % shards_of)
    return jnp.where(strong, factor * result, result)


def block_levels(stream_key, extent, cuts, low, high):
    level = 1.0
    for axis_at, shards_of in cuts:
        heights = jax.random.uniform(jax.random.fold_in(jax.random.fold_in(stream_key, 6), axis_at), (shards_of,), jnp.float32, low / len(cuts), high / len(cuts))
        level = level * jnp.repeat(jnp.exp(heights), extent[axis_at] // shards_of).reshape((-1,) + (1,) * (len(extent) - 1 - axis_at))
    return level


def profile(number_of, total, reach, slope):
    loads = [(1 << 20) // math.isqrt(grade ** slope) + 1 for grade in range(2, number_of + 1)]
    spare, holding = total - reach - (number_of - 1), [1] * (number_of - 1)
    while spare > 0:
        movable = [i for i in range(number_of - 1) if holding[i] < reach]
        whole, budget = sum([loads[i] for i in movable]), spare
        for i in movable:
            addition = min(reach - holding[i], max(1, budget * loads[i] // whole), spare)
            holding[i] = holding[i] + addition
            spare = spare - addition
    return np.array([reach] + holding)


def ragged(stream_key, number_of, total, reach, skew):
    if number_of == 2:
        one = jax.random.randint(stream_key, (), max(1, total - reach), min(reach, total - 1) + 1)
        return jnp.stack([one, total - one])
    sizes = jnp.asarray(profile(number_of, total, reach, skew), jnp.int32)
    couples = (number_of - 1) // 2
    source_of, sink = sizes[1:1 + 2 * couples:2], sizes[2:2 + 2 * couples:2]
    room = jnp.minimum(source_of - 1, reach - sink)
    moved = jax.random.randint(jax.random.fold_in(stream_key, 1), (couples,), 0, 1 << 20) % (room + 1)
    sizes = sizes.at[1:1 + 2 * couples:2].set(source_of - moved).at[2:2 + 2 * couples:2].set(sink + moved)
    return sizes[jax.random.permutation(jax.random.fold_in(stream_key, 2), number_of)]


def scatter_about(own_key, shape, deviation, most, shards=(), held_as=jnp.bfloat16):
    entries = deviation * jax.random.normal(own_key, shape, jnp.float32)
    if shards:
        entries = entries * block_levels(own_key, shape, shards, -0.22, 0.18)
    return jnp.clip(entries, -most, most).astype(held_as)


def gaussian_with(rng, extent, scale, bound, shards, heavy, kind=jnp.bfloat16):
    result = scale * jax.random.normal(rng, extent, jnp.float32)
    if shards:
        result = result * block_levels(rng, extent, shards, -0.22, 0.18)
    return jnp.clip(with_spikes(result, jax.random.fold_in(rng, 3), *heavy), -bound, bound).astype(kind)


def setup_inputs(seed: int = 0) -> dict:
    key_of = jax.random.split(jax.random.key(seed), 7)
    queries = scatter_about(key_of[0], (WINDOW_TOKENS, QUERY_HEADS * HEAD_SIZE), 1.0, 4.0, ((0, 32), (1, 8)))
    rotated_key_rows = scatter_about(key_of[1], (WINDOW_TOKENS, KEY_VALUE_HEADS * HEAD_SIZE), 1.0, 4.0, ((0, 32), (1, 8)))
    value_matrix = scatter_about(key_of[2], (WINDOW_TOKENS, KEY_VALUE_HEADS * HEAD_SIZE), 1.0, 4.0, ((0, 32), (1, 8)))
    out_grad = gaussian_with(key_of[3], (WINDOW_TOKENS, D), 1.0, 6.0, ((0, 32), (1, 8)), (0, 1, 32, 2.75))
    w_out = scatter_about(key_of[4], (QUERY_HEADS * HEAD_SIZE, D), (QUERY_HEADS * HEAD_SIZE) ** -0.5, 0.09375, ((0, 8),))
    doc_lengths = ragged(key_of[5], DOCS, WINDOW_TOKENS, MOST, 2).astype(jnp.int32)
    return {"queries": queries, "rotated_key_rows": rotated_key_rows, "value_matrix": value_matrix, "out_grad": out_grad, "w_out": w_out, "doc_lengths": doc_lengths}


def reference(queries, rotated_key_rows, value_matrix, out_grad, w_out, doc_lengths):
    logit_scale = HEAD_SIZE ** -0.5
    query_group_width = QUERY_HEADS // KEY_VALUE_HEADS
    positions = jnp.arange(WINDOW_TOKENS, dtype=jnp.int32)
    doc_ends = jnp.cumsum(doc_lengths).astype(jnp.int32)
    seg_start = jnp.sum(jnp.where(doc_ends[None, :] <= positions[:, None], doc_lengths[None, :], 0), axis=1).astype(jnp.int32)
    allowed = (positions[None, :] <= positions[:, None]) & (positions[None, :] >= seg_start[:, None])
    grad_attn = lax.dot_general(out_grad, w_out, (((1,), (1,)), ((), ())), preferred_element_type=jnp.float32).astype(jnp.bfloat16)

    def one_head(head_index):
        head_index = head_index.astype(jnp.int32)
        kv_index = head_index // query_group_width
        q_head = lax.dynamic_slice_in_dim(queries, head_index * HEAD_SIZE, HEAD_SIZE, 1)
        k_head = lax.dynamic_slice_in_dim(rotated_key_rows, kv_index * HEAD_SIZE, HEAD_SIZE, 1)
        v_head = lax.dynamic_slice_in_dim(value_matrix, kv_index * HEAD_SIZE, HEAD_SIZE, 1)
        g_head = lax.dynamic_slice_in_dim(grad_attn, head_index * HEAD_SIZE, HEAD_SIZE, 1)
        scores = jnp.dot(q_head, k_head.T, preferred_element_type=jnp.float32) * logit_scale
        expo_vals = jnp.where(allowed, jnp.exp(scores), 0.0)
        totals = jnp.sum(expo_vals, axis=1)
        attn_head = (jnp.dot(expo_vals.astype(jnp.bfloat16), v_head, preferred_element_type=jnp.float32) / totals[:, None]).astype(jnp.bfloat16)
        log_total = jnp.log(totals)
        row_delta = jnp.sum(g_head.astype(jnp.float32) * attn_head.astype(jnp.float32), axis=1)
        attn_weights = jnp.where(allowed, jnp.exp(scores - log_total[:, None]), 0.0)
        grad_weights = jnp.dot(g_head, v_head.T, preferred_element_type=jnp.float32)
        dscore = (attn_weights * (grad_weights - row_delta[:, None])).astype(jnp.bfloat16)
        head_dq = jnp.dot(dscore, k_head, preferred_element_type=jnp.float32)
        head_dk = jnp.dot(dscore.T, q_head, preferred_element_type=jnp.float32)
        head_dv = jnp.dot(attn_weights.astype(jnp.bfloat16).T, g_head, preferred_element_type=jnp.float32)
        return head_dq, head_dk, head_dv, attn_head

    all_dq, key_gradient_rows, value_gradient_rows, attn_all = lax.map(one_head, jnp.arange(QUERY_HEADS, dtype=jnp.int32))
    grad_q = (logit_scale * jnp.transpose(all_dq, (1, 0, 2)).reshape(WINDOW_TOKENS, QUERY_HEADS * HEAD_SIZE)).astype(jnp.bfloat16)
    key_gradient_sum = logit_scale * jnp.sum(key_gradient_rows.reshape(KEY_VALUE_HEADS, query_group_width, WINDOW_TOKENS, HEAD_SIZE), axis=1)
    key_gradient = jnp.transpose(key_gradient_sum, (1, 0, 2)).reshape(WINDOW_TOKENS, KEY_VALUE_HEADS * HEAD_SIZE).astype(jnp.bfloat16)
    value_gradient_sum = jnp.sum(value_gradient_rows.reshape(KEY_VALUE_HEADS, query_group_width, WINDOW_TOKENS, HEAD_SIZE), axis=1)
    value_gradient = jnp.transpose(value_gradient_sum, (1, 0, 2)).reshape(WINDOW_TOKENS, KEY_VALUE_HEADS * HEAD_SIZE).astype(jnp.bfloat16)
    attn_out = jnp.transpose(attn_all, (1, 0, 2)).reshape(WINDOW_TOKENS, QUERY_HEADS * HEAD_SIZE)
    grad_blocks = out_grad.reshape(N_CTX, TOK_DEV, D)
    attn_blocks = attn_out.reshape(N_CTX, TOK_DEV, QUERY_HEADS * HEAD_SIZE)

    def add_block(running, pieces):
        grad_piece, attn_piece = pieces
        partial_sum = lax.dot_general(grad_piece, attn_piece, (((0,), (0,)), ((), ())), preferred_element_type=jnp.float32).astype(jnp.bfloat16)
        return running + partial_sum.astype(jnp.float32), None

    summed_wo, unused = lax.scan(add_block, jnp.zeros((D, QUERY_HEADS * HEAD_SIZE), jnp.float32), (grad_blocks, attn_blocks))
    grad_wo_t = summed_wo.astype(jnp.bfloat16)
    return grad_q, key_gradient, value_gradient, grad_wo_t
```

```python
import jax
import jax.numpy as jnp
from jax import lax
from jax.sharding import PartitionSpec as P

HEAD_SIZE = 128
MOST = 3744


def to_rows(x, kv_heads):
    tok = x.shape[0]
    group = x.shape[1] // (kv_heads * HEAD_SIZE)
    x = x.reshape(tok, kv_heads, group, HEAD_SIZE).transpose(1, 2, 0, 3)
    return x.reshape(kv_heads, group * tok, HEAD_SIZE)


def from_rows(x, tok):
    kv_heads, rows, d = x.shape
    group = rows // tok
    x = x.reshape(kv_heads, group, tok, d).transpose(2, 0, 1, 3)
    return x.reshape(tok, kv_heads * group * d)


def make_per_device(n_ctx):
    def per_device(queries, rotated_key_rows, value_matrix, out_grad, w_out, doc_lengths):
        tok = queries.shape[0]
        kv_heads = rotated_key_rows.shape[1] // HEAD_SIZE
        group = queries.shape[1] // (kv_heads * HEAD_SIZE)
        key_width = kv_heads * HEAD_SIZE
        scale = HEAD_SIZE ** (-0.5)
        back = -(-(MOST - 1) // tok)
        n_slots = min(n_ctx, back + 1)

        me = lax.axis_index("ctx")
        my_first = me * tok
        my_positions = my_first + jnp.arange(tok, dtype=jnp.int32)
        doc_ends = jnp.cumsum(doc_lengths)
        my_segs = jnp.sum(
            jnp.where(doc_ends[None, :] <= my_positions[:, None], doc_lengths[None, :], 0), axis=1
        ).astype(jnp.int32)
        q_pos = jnp.tile(my_positions, group)
        q_seg = jnp.tile(my_segs, group)

        q_rows = to_rows(queries, kv_heads)
        kv_local = jnp.concatenate([rotated_key_rows, value_matrix], axis=1)
        kv_slots = [kv_local]
        for s in range(1, n_slots):
            kv_slots.append(
                lax.ppermute(kv_local, "ctx", [(i, (i + s) % n_ctx) for i in range(n_ctx)])
            )

        grad_cols = lax.all_gather(out_grad, "head", axis=1, tiled=True)

        def slot_parts(s):
            kvs = kv_slots[s]
            k_s = kvs[:, :key_width].reshape(tok, kv_heads, HEAD_SIZE).transpose(1, 0, 2)
            v_s = kvs[:, key_width:].reshape(tok, kv_heads, HEAD_SIZE).transpose(1, 0, 2)
            blk = (me - s) % n_ctx
            key_pos = blk * tok + jnp.arange(tok, dtype=jnp.int32)
            allowed = (key_pos[None, :] <= q_pos[:, None]) & (key_pos[None, :] >= q_seg[:, None])
            scores = (
                jnp.einsum("grd,gkd->grk", q_rows, k_s, preferred_element_type=jnp.float32) * scale
            )
            return k_s, v_s, allowed[None], scores

        weighted = jnp.zeros((kv_heads, group * tok, HEAD_SIZE), jnp.float32)
        totals = jnp.zeros((kv_heads, group * tok), jnp.float32)
        for s in range(n_slots):
            k_s, v_s, allowed, scores = slot_parts(s)
            expo = jnp.where(allowed, jnp.exp(scores), 0.0)
            totals = totals + jnp.sum(expo, axis=2)
            weighted = weighted + jnp.einsum(
                "grk,gkd->grd", expo.astype(jnp.bfloat16), v_s, preferred_element_type=jnp.float32
            )
        attn = (weighted / totals[..., None]).astype(jnp.bfloat16)
        log_total = jnp.log(totals)
        attn_flat = from_rows(attn, tok)

        grad_attn = lax.dot_general(
            grad_cols, w_out, (((1,), (1,)), ((), ())), preferred_element_type=jnp.float32
        ).astype(jnp.bfloat16)
        g_rows = to_rows(grad_attn, kv_heads)
        row_delta = jnp.sum(g_rows.astype(jnp.float32) * attn.astype(jnp.float32), axis=2)

        wo_part = lax.dot_general(
            grad_cols, attn_flat, (((0,), (0,)), ((), ())), preferred_element_type=jnp.float32
        ).astype(jnp.bfloat16)
        wo_rows = wo_part.shape[0] // n_ctx
        wo_recv = lax.all_to_all(
            wo_part.reshape(n_ctx, wo_rows, wo_part.shape[1]), "ctx", 0, 0
        )
        grad_wo = jnp.sum(wo_recv.astype(jnp.float32), axis=0).astype(jnp.bfloat16)

        dq = jnp.zeros((kv_heads, group * tok, HEAD_SIZE), jnp.float32)
        own = None
        received = []
        for s in range(n_slots):
            k_s, v_s, allowed, scores = slot_parts(s)
            weights = jnp.where(allowed, jnp.exp(scores - log_total[..., None]), 0.0)
            grad_weights = jnp.einsum(
                "grd,gkd->grk", g_rows, v_s, preferred_element_type=jnp.float32
            )
            dscore = (weights * (grad_weights - row_delta[..., None])).astype(jnp.bfloat16)
            dq = dq + jnp.einsum("grk,gkd->grd", dscore, k_s, preferred_element_type=jnp.float32)
            dk = jnp.einsum("grk,grd->gkd", dscore, q_rows, preferred_element_type=jnp.float32)
            dv = jnp.einsum(
                "grk,grd->gkd", weights.astype(jnp.bfloat16), g_rows,
                preferred_element_type=jnp.float32,
            )
            part = jnp.concatenate(
                [
                    (scale * dk).transpose(1, 0, 2).reshape(tok, key_width),
                    dv.transpose(1, 0, 2).reshape(tok, key_width),
                ],
                axis=1,
            )
            if s == 0:
                own = part
            else:
                received.append(
                    lax.ppermute(
                        part.astype(jnp.bfloat16),
                        "ctx",
                        [(i, (i - s) % n_ctx) for i in range(n_ctx)],
                    )
                )
        total = own
        for r in received:
            total = total + r.astype(jnp.float32)
        key_gradient = total[:, :key_width].astype(jnp.bfloat16)
        value_gradient = total[:, key_width:].astype(jnp.bfloat16)
        grad_q = from_rows(scale * dq, tok).astype(jnp.bfloat16)
        return (grad_q, key_gradient, value_gradient, grad_wo)

    return per_device


def solution(mesh):
    return jax.shard_map(
        make_per_device(mesh.shape["ctx"]),
        mesh=mesh,
        in_specs=(
            P("ctx", "head"),
            P("ctx", "head"),
            P("ctx", "head"),
            P("ctx", "head"),
            P("head", None),
            P(),
        ),
        out_specs=(P("ctx", "head"), P("ctx", "head"), P("ctx", "head"), P("ctx", "head")),
        check_vma=False,
    )
```

```python
import jax
import jax.numpy as jnp
from jax import lax
from jax.sharding import PartitionSpec as P

HEAD_SIZE = 128
MOST = 3744


def to_rows(x, kv_heads):
    tok = x.shape[0]
    group = x.shape[1] // (kv_heads * HEAD_SIZE)
    x = x.reshape(tok, kv_heads, group, HEAD_SIZE).transpose(1, 2, 0, 3)
    return x.reshape(kv_heads, group * tok, HEAD_SIZE)


def from_rows(x, tok):
    kv_heads, rows, d = x.shape
    group = rows // tok
    x = x.reshape(kv_heads, group, tok, d).transpose(2, 0, 1, 3)
    return x.reshape(tok, kv_heads * group * d)


def make_per_device(n_ctx):
    def per_device(queries, rotated_key_rows, value_matrix, out_grad, w_out, doc_lengths):
        tok = queries.shape[0]
        kv_heads = rotated_key_rows.shape[1] // HEAD_SIZE
        group = queries.shape[1] // (kv_heads * HEAD_SIZE)
        key_width = kv_heads * HEAD_SIZE
        scale = HEAD_SIZE ** (-0.5)
        back = -(-(MOST - 1) // tok)
        n_slots = min(n_ctx, back + 1)

        me = lax.axis_index("ctx")
        my_first = me * tok
        my_positions = my_first + jnp.arange(tok, dtype=jnp.int32)
        doc_ends = jnp.cumsum(doc_lengths)
        my_segs = jnp.sum(
            jnp.where(doc_ends[None, :] <= my_positions[:, None], doc_lengths[None, :], 0), axis=1
        ).astype(jnp.int32)
        q_pos = jnp.tile(my_positions, group)
        q_seg = jnp.tile(my_segs, group)

        q_rows = to_rows(queries, kv_heads)
        kv_local = jnp.concatenate([rotated_key_rows, value_matrix], axis=1)
        kv_slots = [kv_local]
        for s in range(1, n_slots):
            kv_slots.append(
                lax.ppermute(kv_local, "ctx", [(i, (i + s) % n_ctx) for i in range(n_ctx)])
            )

        grad_cols = lax.all_gather(out_grad, "head", axis=1, tiled=True)

        def slot_parts(s):
            kvs = kv_slots[s]
            k_s = kvs[:, :key_width].reshape(tok, kv_heads, HEAD_SIZE).transpose(1, 0, 2)
            v_s = kvs[:, key_width:].reshape(tok, kv_heads, HEAD_SIZE).transpose(1, 0, 2)
            blk = (me - s) % n_ctx
            key_pos = blk * tok + jnp.arange(tok, dtype=jnp.int32)
            allowed = (key_pos[None, :] <= q_pos[:, None]) & (key_pos[None, :] >= q_seg[:, None])
            scores = (
                jnp.einsum("grd,gkd->grk", q_rows, k_s, preferred_element_type=jnp.float32) * scale
            )
            return k_s, v_s, allowed[None], scores

        weighted = jnp.zeros((kv_heads, group * tok, HEAD_SIZE), jnp.float32)
        totals = jnp.zeros((kv_heads, group * tok), jnp.float32)
        for s in range(n_slots):
            k_s, v_s, allowed, scores = slot_parts(s)
            expo = jnp.where(allowed, jnp.exp(scores), 0.0)
            totals = totals + jnp.sum(expo, axis=2)
            weighted = weighted + jnp.einsum(
                "grk,gkd->grd", expo.astype(jnp.bfloat16), v_s, preferred_element_type=jnp.float32
            )
        attn = (weighted / totals[..., None]).astype(jnp.bfloat16)
        log_total = jnp.log(totals)
        attn_flat = from_rows(attn, tok)

        grad_attn = lax.dot_general(
            grad_cols, w_out, (((1,), (1,)), ((), ())), preferred_element_type=jnp.float32
        ).astype(jnp.bfloat16)
        g_rows = to_rows(grad_attn, kv_heads)
        row_delta = jnp.sum(g_rows.astype(jnp.float32) * attn.astype(jnp.float32), axis=2)

        wo_part = lax.dot_general(
            grad_cols, attn_flat, (((0,), (0,)), ((), ())), preferred_element_type=jnp.float32
        ).astype(jnp.bfloat16)
        wo_part, g_rows, row_delta = lax.optimization_barrier((wo_part, g_rows, row_delta))
        grad_wo = lax.psum_scatter(wo_part, "ctx", scatter_dimension=0, tiled=True)

        dq = jnp.zeros((kv_heads, group * tok, HEAD_SIZE), jnp.float32)
        own = None
        received = []
        for s in range(n_slots):
            k_s, v_s, allowed, scores = slot_parts(s)
            weights = jnp.where(allowed, jnp.exp(scores - log_total[..., None]), 0.0)
            grad_weights = jnp.einsum(
                "grd,gkd->grk", g_rows, v_s, preferred_element_type=jnp.float32
            )
            dscore = (weights * (grad_weights - row_delta[..., None])).astype(jnp.bfloat16)
            dq = dq + jnp.einsum("grk,gkd->grd", dscore, k_s, preferred_element_type=jnp.float32)
            dk = jnp.einsum("grk,grd->gkd", dscore, q_rows, preferred_element_type=jnp.float32)
            dv = jnp.einsum(
                "grk,grd->gkd", weights.astype(jnp.bfloat16), g_rows,
                preferred_element_type=jnp.float32,
            )
            part = jnp.concatenate(
                [
                    (scale * dk).transpose(1, 0, 2).reshape(tok, key_width),
                    dv.transpose(1, 0, 2).reshape(tok, key_width),
                ],
                axis=1,
            )
            if s == 0:
                own = part
            else:
                received.append(
                    lax.ppermute(
                        part.astype(jnp.bfloat16),
                        "ctx",
                        [(i, (i - s) % n_ctx) for i in range(n_ctx)],
                    )
                )
        total = own
        for r in received:
            total = total + r.astype(jnp.float32)
        key_gradient = total[:, :key_width].astype(jnp.bfloat16)
        value_gradient = total[:, key_width:].astype(jnp.bfloat16)
        grad_q = from_rows(scale * dq, tok).astype(jnp.bfloat16)
        return (grad_q, key_gradient, value_gradient, grad_wo)

    return per_device


def solution(mesh):
    return jax.shard_map(
        make_per_device(mesh.shape["ctx"]),
        mesh=mesh,
        in_specs=(
            P("ctx", "head"),
            P("ctx", "head"),
            P("ctx", "head"),
            P("ctx", "head"),
            P("head", None),
            P(),
        ),
        out_specs=(P("ctx", "head"), P("ctx", "head"), P("ctx", "head"), P("ctx", "head")),
        check_vma=False,
    )
```

```python
import jax
import jax.numpy as jnp
from jax import lax
from jax.sharding import PartitionSpec as P

HEAD_SIZE = 128
MOST = 3744


def to_rows(x, kv_heads):
    tok = x.shape[0]
    group = x.shape[1] // (kv_heads * HEAD_SIZE)
    x = x.reshape(tok, kv_heads, group, HEAD_SIZE).transpose(1, 2, 0, 3)
    return x.reshape(kv_heads, group * tok, HEAD_SIZE)


def from_rows(x, tok):
    kv_heads, rows, d = x.shape
    group = rows // tok
    x = x.reshape(kv_heads, group, tok, d).transpose(2, 0, 1, 3)
    return x.reshape(tok, kv_heads * group * d)


def make_per_device(n_ctx):
    def per_device(queries, rotated_key_rows, value_matrix, out_grad, w_out, doc_lengths):
        tok = queries.shape[0]
        kv_heads = rotated_key_rows.shape[1] // HEAD_SIZE
        group = queries.shape[1] // (kv_heads * HEAD_SIZE)
        key_width = kv_heads * HEAD_SIZE
        scale = HEAD_SIZE ** (-0.5)
        back = -(-(MOST - 1) // tok)
        n_slots = min(n_ctx, back + 1)

        me = lax.axis_index("ctx")
        my_first = me * tok
        my_positions = my_first + jnp.arange(tok, dtype=jnp.int32)
        doc_ends = jnp.cumsum(doc_lengths)
        my_segs = jnp.sum(
            jnp.where(doc_ends[None, :] <= my_positions[:, None], doc_lengths[None, :], 0), axis=1
        ).astype(jnp.int32)
        q_pos = jnp.tile(my_positions, group)
        q_seg = jnp.tile(my_segs, group)

        q_rows = to_rows(queries, kv_heads)
        kv_local = jnp.concatenate([rotated_key_rows, value_matrix], axis=1)

        def shifted(x, shift):
            return lax.ppermute(x, "ctx", [(i, (i + shift) % n_ctx) for i in range(n_ctx)])

        kv_slots = [kv_local]
        width = 1
        while width < min(n_slots, 4):
            take = min(width, n_slots - width)
            got = shifted(jnp.concatenate(kv_slots[:take], axis=0), width)
            kv_slots += [got[i * tok:(i + 1) * tok] for i in range(take)]
            width *= 2
        base = jnp.concatenate(kv_slots[:width], axis=0)
        for shift in range(width, n_slots, width):
            take = min(width, n_slots - shift)
            got = shifted(base[: take * tok], shift)
            kv_slots += [got[i * tok:(i + 1) * tok] for i in range(take)]

        grad_cols = lax.all_gather(out_grad, "head", axis=1, tiled=True)

        def slot_parts(s):
            kvs = kv_slots[s]
            k_s = kvs[:, :key_width].reshape(tok, kv_heads, HEAD_SIZE).transpose(1, 0, 2)
            v_s = kvs[:, key_width:].reshape(tok, kv_heads, HEAD_SIZE).transpose(1, 0, 2)
            blk = (me - s) % n_ctx
            key_pos = blk * tok + jnp.arange(tok, dtype=jnp.int32)
            allowed = (key_pos[None, :] <= q_pos[:, None]) & (key_pos[None, :] >= q_seg[:, None])
            scores = (
                jnp.einsum("grd,gkd->grk", q_rows, k_s, preferred_element_type=jnp.float32) * scale
            )
            return k_s, v_s, allowed[None], scores

        weighted = jnp.zeros((kv_heads, group * tok, HEAD_SIZE), jnp.float32)
        totals = jnp.zeros((kv_heads, group * tok), jnp.float32)
        for s in range(n_slots):
            k_s, v_s, allowed, scores = slot_parts(s)
            expo = jnp.where(allowed, jnp.exp(scores), 0.0)
            totals = totals + jnp.sum(expo, axis=2)
            weighted = weighted + jnp.einsum(
                "grk,gkd->grd", expo.astype(jnp.bfloat16), v_s, preferred_element_type=jnp.float32
            )
        attn = (weighted / totals[..., None]).astype(jnp.bfloat16)
        log_total = jnp.log(totals)
        attn_flat = from_rows(attn, tok)

        grad_attn = lax.dot_general(
            grad_cols, w_out, (((1,), (1,)), ((), ())), preferred_element_type=jnp.float32
        ).astype(jnp.bfloat16)
        g_rows = to_rows(grad_attn, kv_heads)
        row_delta = jnp.sum(g_rows.astype(jnp.float32) * attn.astype(jnp.float32), axis=2)

        wo_part = lax.dot_general(
            grad_cols, attn_flat, (((0,), (0,)), ((), ())), preferred_element_type=jnp.float32
        ).astype(jnp.bfloat16)
        wo_part, g_rows, row_delta = lax.optimization_barrier((wo_part, g_rows, row_delta))
        grad_wo = lax.psum_scatter(wo_part, "ctx", scatter_dimension=0, tiled=True)

        dq = jnp.zeros((kv_heads, group * tok, HEAD_SIZE), jnp.float32)
        parts = [None] * n_slots
        for s in reversed(range(n_slots)):
            k_s, v_s, allowed, scores = slot_parts(s)
            weights = jnp.where(allowed, jnp.exp(scores - log_total[..., None]), 0.0)
            grad_weights = jnp.einsum(
                "grd,gkd->grk", g_rows, v_s, preferred_element_type=jnp.float32
            )
            dscore = (weights * (grad_weights - row_delta[..., None])).astype(jnp.bfloat16)
            dq = dq + jnp.einsum("grk,gkd->grd", dscore, k_s, preferred_element_type=jnp.float32)
            dk = jnp.einsum("grk,grd->gkd", dscore, q_rows, preferred_element_type=jnp.float32)
            dv = jnp.einsum(
                "grk,grd->gkd", weights.astype(jnp.bfloat16), g_rows,
                preferred_element_type=jnp.float32,
            )
            part = jnp.concatenate(
                [
                    (scale * dk).transpose(1, 0, 2).reshape(tok, key_width),
                    dv.transpose(1, 0, 2).reshape(tok, key_width),
                ],
                axis=1,
            )
            parts[s] = part
        acc = parts[:width]
        for shift in range(width, n_slots, width):
            take = min(width, n_slots - shift)
            sent = jnp.concatenate(parts[shift:shift + take], axis=0).astype(jnp.bfloat16)
            got = shifted(sent, -shift).astype(jnp.float32)
            for i in range(take):
                acc[i] = acc[i] + got[i * tok:(i + 1) * tok]
        while width > 1:
            width //= 2
            take = min(width, len(acc) - width)
            sent = jnp.concatenate(acc[width:width + take], axis=0).astype(jnp.bfloat16)
            got = shifted(sent, -width).astype(jnp.float32)
            acc = [acc[i] + got[i * tok:(i + 1) * tok] if i < take else acc[i] for i in range(width)]
        total = acc[0]
        key_gradient = total[:, :key_width].astype(jnp.bfloat16)
        value_gradient = total[:, key_width:].astype(jnp.bfloat16)
        grad_q = from_rows(scale * dq, tok).astype(jnp.bfloat16)
        return (grad_q, key_gradient, value_gradient, grad_wo)

    return per_device


def solution(mesh):
    return jax.shard_map(
        make_per_device(mesh.shape["ctx"]),
        mesh=mesh,
        in_specs=(
            P("ctx", "head"),
            P("ctx", "head"),
            P("ctx", "head"),
            P("ctx", "head"),
            P("head", None),
            P(),
        ),
        out_specs=(P("ctx", "head"), P("ctx", "head"), P("ctx", "head"), P("ctx", "head")),
        check_vma=False,
    )
```

```python
import jax
import jax.numpy as jnp
from jax import lax
from jax.sharding import PartitionSpec as P

HEAD_SIZE = 128
MOST = 3744


def to_rows(x, kv_heads):
    tok = x.shape[0]
    group = x.shape[1] // (kv_heads * HEAD_SIZE)
    x = x.reshape(tok, kv_heads, group, HEAD_SIZE).transpose(1, 2, 0, 3)
    return x.reshape(kv_heads, group * tok, HEAD_SIZE)


def from_rows(x, tok):
    kv_heads, rows, d = x.shape
    group = rows // tok
    x = x.reshape(kv_heads, group, tok, d).transpose(2, 0, 1, 3)
    return x.reshape(tok, kv_heads * group * d)


def make_per_device(n_ctx):
    def per_device(queries, rotated_key_rows, value_matrix, out_grad, w_out, doc_lengths):
        tok = queries.shape[0]
        kv_heads = rotated_key_rows.shape[1] // HEAD_SIZE
        group = queries.shape[1] // (kv_heads * HEAD_SIZE)
        key_width = kv_heads * HEAD_SIZE
        scale = HEAD_SIZE ** (-0.5)
        back = -(-(MOST - 1) // tok)
        n_slots = min(n_ctx, back + 1)

        me = lax.axis_index("ctx")
        my_first = me * tok
        my_positions = my_first + jnp.arange(tok, dtype=jnp.int32)
        doc_ends = jnp.cumsum(doc_lengths)
        my_segs = jnp.sum(
            jnp.where(doc_ends[None, :] <= my_positions[:, None], doc_lengths[None, :], 0), axis=1
        ).astype(jnp.int32)
        q_pos = jnp.tile(my_positions, group)
        q_seg = jnp.tile(my_segs, group)

        q_rows = to_rows(queries, kv_heads)
        kv_local = jnp.concatenate([rotated_key_rows, value_matrix], axis=1)

        def shifted(x, shift):
            return lax.ppermute(x, "ctx", [(i, (i + shift) % n_ctx) for i in range(n_ctx)])

        kv_slots = [kv_local]
        width = 1
        while width < min(n_slots, 4):
            take = min(width, n_slots - width)
            got = shifted(jnp.concatenate(kv_slots[:take], axis=0), width)
            kv_slots += [got[i * tok:(i + 1) * tok] for i in range(take)]
            width *= 2
        base = jnp.concatenate(kv_slots[:width], axis=0)
        for shift in range(width, n_slots, width):
            take = min(width, n_slots - shift)
            got = shifted(base[: take * tok], shift)
            kv_slots += [got[i * tok:(i + 1) * tok] for i in range(take)]

        grad_cols = lax.all_gather(out_grad, "head", axis=1, tiled=True)

        def slot_parts(s):
            kvs = kv_slots[s]
            k_s = kvs[:, :key_width].reshape(tok, kv_heads, HEAD_SIZE).transpose(1, 0, 2)
            v_s = kvs[:, key_width:].reshape(tok, kv_heads, HEAD_SIZE).transpose(1, 0, 2)
            blk = (me - s) % n_ctx
            key_pos = blk * tok + jnp.arange(tok, dtype=jnp.int32)
            allowed = (key_pos[None, :] <= q_pos[:, None]) & (key_pos[None, :] >= q_seg[:, None])
            scores = (
                jnp.einsum("grd,gkd->grk", q_rows, k_s, preferred_element_type=jnp.float32) * scale
            )
            return k_s, v_s, allowed[None], scores

        weighted = jnp.zeros((kv_heads, group * tok, HEAD_SIZE), jnp.float32)
        totals = jnp.zeros((kv_heads, group * tok), jnp.float32)
        for s in range(n_slots):
            k_s, v_s, allowed, scores = slot_parts(s)
            expo = jnp.where(allowed, jnp.exp(scores), 0.0)
            totals = totals + jnp.sum(expo, axis=2)
            weighted = weighted + jnp.einsum(
                "grk,gkd->grd", expo.astype(jnp.bfloat16), v_s, preferred_element_type=jnp.float32
            )
        attn = (weighted / totals[..., None]).astype(jnp.bfloat16)
        log_total = jnp.log(totals)
        attn_flat = from_rows(attn, tok)

        grad_attn = lax.dot_general(
            grad_cols, w_out, (((1,), (1,)), ((), ())), preferred_element_type=jnp.float32
        ).astype(jnp.bfloat16)
        g_rows = to_rows(grad_attn, kv_heads)
        row_delta = jnp.sum(g_rows.astype(jnp.float32) * attn.astype(jnp.float32), axis=2)

        wo_part = lax.dot_general(
            grad_cols, attn_flat, (((0,), (0,)), ((), ())), preferred_element_type=jnp.float32
        ).astype(jnp.bfloat16)
        wo_part, g_rows, row_delta = lax.optimization_barrier((wo_part, g_rows, row_delta))
        split = wo_part.shape[1] // 2
        wo_sc = lax.psum_scatter(wo_part[:, :split], "ctx", scatter_dimension=0, tiled=True)
        wo_rows = wo_part.shape[0] // n_ctx
        cur = wo_part[:, split:].reshape(n_ctx, wo_rows, wo_part.shape[1] - split)
        bit = 1
        while bit < n_ctx:
            pair = cur.reshape(cur.shape[0] // 2, 2, wo_rows, cur.shape[2])
            mine = (me // bit) % 2
            keep = lax.dynamic_index_in_dim(pair, mine, axis=1, keepdims=False)
            away = lax.dynamic_index_in_dim(pair, 1 - mine, axis=1, keepdims=False)
            got = lax.ppermute(
                away.astype(jnp.bfloat16), "ctx", [(i, i ^ bit) for i in range(n_ctx)]
            )
            cur = keep.astype(jnp.float32) + got.astype(jnp.float32)
            bit *= 2
        grad_wo = jnp.concatenate([wo_sc, cur[0].astype(jnp.bfloat16)], axis=1)

        dq = jnp.zeros((kv_heads, group * tok, HEAD_SIZE), jnp.float32)
        parts = [None] * n_slots
        for s in reversed(range(n_slots)):
            k_s, v_s, allowed, scores = slot_parts(s)
            weights = jnp.where(allowed, jnp.exp(scores - log_total[..., None]), 0.0)
            grad_weights = jnp.einsum(
                "grd,gkd->grk", g_rows, v_s, preferred_element_type=jnp.float32
            )
            dscore = (weights * (grad_weights - row_delta[..., None])).astype(jnp.bfloat16)
            dq = dq + jnp.einsum("grk,gkd->grd", dscore, k_s, preferred_element_type=jnp.float32)
            dk = jnp.einsum("grk,grd->gkd", dscore, q_rows, preferred_element_type=jnp.float32)
            dv = jnp.einsum(
                "grk,grd->gkd", weights.astype(jnp.bfloat16), g_rows,
                preferred_element_type=jnp.float32,
            )
            part = jnp.concatenate(
                [
                    (scale * dk).transpose(1, 0, 2).reshape(tok, key_width),
                    dv.transpose(1, 0, 2).reshape(tok, key_width),
                ],
                axis=1,
            )
            parts[s] = part
        acc = parts[:width]
        for shift in range(width, n_slots, width):
            take = min(width, n_slots - shift)
            sent = jnp.concatenate(parts[shift:shift + take], axis=0).astype(jnp.bfloat16)
            got = shifted(sent, -shift).astype(jnp.float32)
            for i in range(take):
                acc[i] = acc[i] + got[i * tok:(i + 1) * tok]
        while width > 1:
            width //= 2
            take = min(width, len(acc) - width)
            sent = jnp.concatenate(acc[width:width + take], axis=0).astype(jnp.bfloat16)
            got = shifted(sent, -width).astype(jnp.float32)
            acc = [acc[i] + got[i * tok:(i + 1) * tok] if i < take else acc[i] for i in range(width)]
        total = acc[0]
        key_gradient = total[:, :key_width].astype(jnp.bfloat16)
        value_gradient = total[:, key_width:].astype(jnp.bfloat16)
        grad_q = from_rows(scale * dq, tok).astype(jnp.bfloat16)
        return (grad_q, key_gradient, value_gradient, grad_wo)

    return per_device


def solution(mesh):
    return jax.shard_map(
        make_per_device(mesh.shape["ctx"]),
        mesh=mesh,
        in_specs=(
            P("ctx", "head"),
            P("ctx", "head"),
            P("ctx", "head"),
            P("ctx", "head"),
            P("head", None),
            P(),
        ),
        out_specs=(P("ctx", "head"), P("ctx", "head"), P("ctx", "head"), P("ctx", "head")),
        check_vma=False,
    )
```

```python
import jax
import jax.numpy as jnp
from jax import lax
from jax.sharding import PartitionSpec as P

HEAD_SIZE = 128
MOST = 3744
CTX_PARTS = ("ctx_x", "ctx_z", "ctx_core")


def to_rows(x, kv_heads):
    tok = x.shape[0]
    group = x.shape[1] // (kv_heads * HEAD_SIZE)
    x = x.reshape(tok, kv_heads, group, HEAD_SIZE).transpose(1, 2, 0, 3)
    return x.reshape(kv_heads, group * tok, HEAD_SIZE)


def from_rows(x, tok):
    kv_heads, rows, d = x.shape
    group = rows // tok
    x = x.reshape(kv_heads, group, tok, d).transpose(2, 0, 1, 3)
    return x.reshape(tok, kv_heads * group * d)


def make_per_device(n_ctx):
    def per_device(queries, rotated_key_rows, value_matrix, out_grad, w_out, doc_lengths):
        tok = queries.shape[0]
        kv_heads = rotated_key_rows.shape[1] // HEAD_SIZE
        group = queries.shape[1] // (kv_heads * HEAD_SIZE)
        key_width = kv_heads * HEAD_SIZE
        scale = HEAD_SIZE ** (-0.5)
        back = -(-(MOST - 1) // tok)
        n_slots = min(n_ctx, back + 1)

        me = lax.axis_index(CTX_PARTS)
        my_first = me * tok
        my_positions = my_first + jnp.arange(tok, dtype=jnp.int32)
        doc_ends = jnp.cumsum(doc_lengths)
        my_segs = jnp.sum(
            jnp.where(doc_ends[None, :] <= my_positions[:, None], doc_lengths[None, :], 0), axis=1
        ).astype(jnp.int32)
        q_pos = jnp.tile(my_positions, group)
        q_seg = jnp.tile(my_segs, group)

        q_rows = to_rows(queries, kv_heads)
        kv_local = jnp.concatenate([rotated_key_rows, value_matrix], axis=1)

        def shifted(x, shift):
            return lax.ppermute(x, CTX_PARTS, [(i, (i + shift) % n_ctx) for i in range(n_ctx)])

        kv_slots = [kv_local]
        width = 1
        while width < min(n_slots, 4):
            take = min(width, n_slots - width)
            got = shifted(jnp.concatenate(kv_slots[:take], axis=0), width)
            kv_slots += [got[i * tok:(i + 1) * tok] for i in range(take)]
            width *= 2
        base = jnp.concatenate(kv_slots[:width], axis=0)
        for shift in range(width, n_slots, width):
            take = min(width, n_slots - shift)
            got = shifted(base[: take * tok], shift)
            kv_slots += [got[i * tok:(i + 1) * tok] for i in range(take)]

        grad_cols = lax.all_gather(out_grad, "head", axis=1, tiled=True)

        def slot_parts(s):
            kvs = kv_slots[s]
            k_s = kvs[:, :key_width].reshape(tok, kv_heads, HEAD_SIZE).transpose(1, 0, 2)
            v_s = kvs[:, key_width:].reshape(tok, kv_heads, HEAD_SIZE).transpose(1, 0, 2)
            blk = (me - s) % n_ctx
            key_pos = blk * tok + jnp.arange(tok, dtype=jnp.int32)
            allowed = (key_pos[None, :] <= q_pos[:, None]) & (key_pos[None, :] >= q_seg[:, None])
            scores = (
                jnp.einsum("grd,gkd->grk", q_rows, k_s, preferred_element_type=jnp.float32) * scale
            )
            return k_s, v_s, allowed[None], scores

        weighted = jnp.zeros((kv_heads, group * tok, HEAD_SIZE), jnp.float32)
        totals = jnp.zeros((kv_heads, group * tok), jnp.float32)
        for s in range(n_slots):
            k_s, v_s, allowed, scores = slot_parts(s)
            expo = jnp.where(allowed, jnp.exp(scores), 0.0)
            totals = totals + jnp.sum(expo, axis=2)
            weighted = weighted + jnp.einsum(
                "grk,gkd->grd", expo.astype(jnp.bfloat16), v_s, preferred_element_type=jnp.float32
            )
        attn = (weighted / totals[..., None]).astype(jnp.bfloat16)
        log_total = jnp.log(totals)
        attn_flat = from_rows(attn, tok)

        grad_attn = lax.dot_general(
            grad_cols, w_out, (((1,), (1,)), ((), ())), preferred_element_type=jnp.float32
        ).astype(jnp.bfloat16)
        g_rows = to_rows(grad_attn, kv_heads)
        row_delta = jnp.sum(g_rows.astype(jnp.float32) * attn.astype(jnp.float32), axis=2)

        wo_part = lax.dot_general(
            grad_cols, attn_flat, (((0,), (0,)), ((), ())), preferred_element_type=jnp.float32
        ).astype(jnp.bfloat16)
        wo_part, g_rows, row_delta = lax.optimization_barrier((wo_part, g_rows, row_delta))
        wo_rows = wo_part.shape[0] // n_ctx
        sizes = [lax.axis_size(a) for a in CTX_PARTS]
        staged = wo_part.reshape(*sizes, wo_rows, wo_part.shape[1])
        staged = staged.transpose(*reversed(range(len(sizes))), len(sizes), len(sizes) + 1)
        staged = staged.reshape(wo_part.shape)
        for a in reversed(CTX_PARTS):
            staged = lax.psum_scatter(staged, a, scatter_dimension=0, tiled=True)
        grad_wo = staged

        dq = jnp.zeros((kv_heads, group * tok, HEAD_SIZE), jnp.float32)
        parts = [None] * n_slots
        for s in reversed(range(n_slots)):
            k_s, v_s, allowed, scores = slot_parts(s)
            weights = jnp.where(allowed, jnp.exp(scores - log_total[..., None]), 0.0)
            grad_weights = jnp.einsum(
                "grd,gkd->grk", g_rows, v_s, preferred_element_type=jnp.float32
            )
            dscore = (weights * (grad_weights - row_delta[..., None])).astype(jnp.bfloat16)
            dq = dq + jnp.einsum("grk,gkd->grd", dscore, k_s, preferred_element_type=jnp.float32)
            dk = jnp.einsum("grk,grd->gkd", dscore, q_rows, preferred_element_type=jnp.float32)
            dv = jnp.einsum(
                "grk,grd->gkd", weights.astype(jnp.bfloat16), g_rows,
                preferred_element_type=jnp.float32,
            )
            part = jnp.concatenate(
                [
                    (scale * dk).transpose(1, 0, 2).reshape(tok, key_width),
                    dv.transpose(1, 0, 2).reshape(tok, key_width),
                ],
                axis=1,
            )
            parts[s] = part
        acc = parts[:width]
        for shift in range(width, n_slots, width):
            take = min(width, n_slots - shift)
            sent = jnp.concatenate(parts[shift:shift + take], axis=0).astype(jnp.bfloat16)
            got = shifted(sent, -shift).astype(jnp.float32)
            for i in range(take):
                acc[i] = acc[i] + got[i * tok:(i + 1) * tok]
        while width > 1:
            width //= 2
            take = min(width, len(acc) - width)
            sent = jnp.concatenate(acc[width:width + take], axis=0).astype(jnp.bfloat16)
            got = shifted(sent, -width).astype(jnp.float32)
            acc = [acc[i] + got[i * tok:(i + 1) * tok] if i < take else acc[i] for i in range(width)]
        total = acc[0]
        key_gradient = total[:, :key_width].astype(jnp.bfloat16)
        value_gradient = total[:, key_width:].astype(jnp.bfloat16)
        grad_q = from_rows(scale * dq, tok).astype(jnp.bfloat16)
        return (grad_q, key_gradient, value_gradient, grad_wo)

    return per_device


def solution(mesh):
    devs = mesh.devices.reshape(2, mesh.shape["ctx"] // 4, 2, mesh.shape["head"])
    sub_mesh = jax.sharding.Mesh(devs, CTX_PARTS + ("head",))
    return jax.shard_map(
        make_per_device(mesh.shape["ctx"]),
        mesh=sub_mesh,
        in_specs=(
            P(CTX_PARTS, "head"),
            P(CTX_PARTS, "head"),
            P(CTX_PARTS, "head"),
            P(CTX_PARTS, "head"),
            P("head", None),
            P(),
        ),
        out_specs=(P(CTX_PARTS, "head"), P(CTX_PARTS, "head"), P(CTX_PARTS, "head"), P(CTX_PARTS, "head")),
        check_vma=False,
    )
```

```python
import jax
import jax.numpy as jnp
from jax import lax
from jax.sharding import PartitionSpec as P

HEAD_SIZE = 128
MOST = 3744
CTX_PARTS = ("ctx_x", "ctx_z", "ctx_core")


def to_rows(x, kv_heads):
    tok = x.shape[0]
    group = x.shape[1] // (kv_heads * HEAD_SIZE)
    x = x.reshape(tok, kv_heads, group, HEAD_SIZE).transpose(1, 2, 0, 3)
    return x.reshape(kv_heads, group * tok, HEAD_SIZE)


def from_rows(x, tok):
    kv_heads, rows, d = x.shape
    group = rows // tok
    x = x.reshape(kv_heads, group, tok, d).transpose(2, 0, 1, 3)
    return x.reshape(tok, kv_heads * group * d)


def make_per_device(n_ctx):
    def per_device(queries, rotated_key_rows, value_matrix, out_grad, w_out, doc_lengths):
        tok = queries.shape[0]
        kv_heads = rotated_key_rows.shape[1] // HEAD_SIZE
        group = queries.shape[1] // (kv_heads * HEAD_SIZE)
        key_width = kv_heads * HEAD_SIZE
        scale = HEAD_SIZE ** (-0.5)
        back = -(-(MOST - 1) // tok)
        n_slots = min(n_ctx, back + 1)

        me = lax.axis_index(CTX_PARTS)
        my_first = me * tok
        my_positions = my_first + jnp.arange(tok, dtype=jnp.int32)
        doc_ends = jnp.cumsum(doc_lengths)
        my_segs = jnp.sum(
            jnp.where(doc_ends[None, :] <= my_positions[:, None], doc_lengths[None, :], 0), axis=1
        ).astype(jnp.int32)
        q_pos = jnp.tile(my_positions, group)
        q_seg = jnp.tile(my_segs, group)

        q_rows = to_rows(queries, kv_heads)
        kv_local = jnp.concatenate([rotated_key_rows, value_matrix], axis=1)

        def shifted(x, shift):
            return lax.ppermute(x, CTX_PARTS, [(i, (i + shift) % n_ctx) for i in range(n_ctx)])

        kv_slots = [kv_local]
        width = 1
        while width < min(n_slots, 4):
            take = min(width, n_slots - width)
            got = shifted(jnp.concatenate(kv_slots[:take], axis=0), width)
            kv_slots += [got[i * tok:(i + 1) * tok] for i in range(take)]
            width *= 2
        base = jnp.concatenate(kv_slots[:width], axis=0)
        for shift in range(width, n_slots, width):
            take = min(width, n_slots - shift)
            got = shifted(base[: take * tok], shift)
            kv_slots += [got[i * tok:(i + 1) * tok] for i in range(take)]

        grad_cols = lax.all_gather(out_grad, "head", axis=1, tiled=True)

        def slot_parts(s):
            kvs = kv_slots[s]
            k_s = kvs[:, :key_width].reshape(tok, kv_heads, HEAD_SIZE).transpose(1, 0, 2)
            v_s = kvs[:, key_width:].reshape(tok, kv_heads, HEAD_SIZE).transpose(1, 0, 2)
            blk = (me - s) % n_ctx
            key_pos = blk * tok + jnp.arange(tok, dtype=jnp.int32)
            allowed = (key_pos[None, :] <= q_pos[:, None]) & (key_pos[None, :] >= q_seg[:, None])
            scores = (
                jnp.einsum("grd,gkd->grk", q_rows, k_s, preferred_element_type=jnp.float32) * scale
            )
            return k_s, v_s, allowed[None], scores

        weighted = jnp.zeros((kv_heads, group * tok, HEAD_SIZE), jnp.float32)
        totals = jnp.zeros((kv_heads, group * tok), jnp.float32)
        for s in range(n_slots):
            k_s, v_s, allowed, scores = slot_parts(s)
            expo = jnp.where(allowed, jnp.exp(scores), 0.0)
            totals = totals + jnp.sum(expo, axis=2)
            weighted = weighted + jnp.einsum(
                "grk,gkd->grd", expo.astype(jnp.bfloat16), v_s, preferred_element_type=jnp.float32
            )
        attn = (weighted / totals[..., None]).astype(jnp.bfloat16)
        log_total = jnp.log(totals)
        attn_flat = from_rows(attn, tok)

        grad_attn = lax.dot_general(
            grad_cols, w_out, (((1,), (1,)), ((), ())), preferred_element_type=jnp.float32
        ).astype(jnp.bfloat16)
        g_rows = to_rows(grad_attn, kv_heads)
        row_delta = jnp.sum(g_rows.astype(jnp.float32) * attn.astype(jnp.float32), axis=2)

        wo_part = lax.dot_general(
            grad_cols, attn_flat, (((0,), (0,)), ((), ())), preferred_element_type=jnp.float32
        ).astype(jnp.bfloat16)
        wo_part, g_rows, row_delta = lax.optimization_barrier((wo_part, g_rows, row_delta))
        wo_rows = wo_part.shape[0] // n_ctx
        outer = n_ctx // lax.axis_size(CTX_PARTS[-1])
        staged = wo_part.reshape(outer, lax.axis_size(CTX_PARTS[-1]), wo_rows, wo_part.shape[1])
        staged = staged.transpose(1, 0, 2, 3).reshape(wo_part.shape)
        staged = lax.psum_scatter(staged, CTX_PARTS[-1], scatter_dimension=0, tiled=True)
        grad_wo = lax.psum_scatter(staged, CTX_PARTS[:-1], scatter_dimension=0, tiled=True)

        dq = jnp.zeros((kv_heads, group * tok, HEAD_SIZE), jnp.float32)
        parts = [None] * n_slots
        for s in reversed(range(n_slots)):
            k_s, v_s, allowed, scores = slot_parts(s)
            weights = jnp.where(allowed, jnp.exp(scores - log_total[..., None]), 0.0)
            grad_weights = jnp.einsum(
                "grd,gkd->grk", g_rows, v_s, preferred_element_type=jnp.float32
            )
            dscore = (weights * (grad_weights - row_delta[..., None])).astype(jnp.bfloat16)
            dq = dq + jnp.einsum("grk,gkd->grd", dscore, k_s, preferred_element_type=jnp.float32)
            dk = jnp.einsum("grk,grd->gkd", dscore, q_rows, preferred_element_type=jnp.float32)
            dv = jnp.einsum(
                "grk,grd->gkd", weights.astype(jnp.bfloat16), g_rows,
                preferred_element_type=jnp.float32,
            )
            part = jnp.concatenate(
                [
                    (scale * dk).transpose(1, 0, 2).reshape(tok, key_width),
                    dv.transpose(1, 0, 2).reshape(tok, key_width),
                ],
                axis=1,
            )
            parts[s] = part
        acc = parts[:width]
        for shift in range(width, n_slots, width):
            take = min(width, n_slots - shift)
            sent = jnp.concatenate(parts[shift:shift + take], axis=0).astype(jnp.bfloat16)
            got = shifted(sent, -shift).astype(jnp.float32)
            for i in range(take):
                acc[i] = acc[i] + got[i * tok:(i + 1) * tok]
        while width > 1:
            width //= 2
            take = min(width, len(acc) - width)
            sent = jnp.concatenate(acc[width:width + take], axis=0).astype(jnp.bfloat16)
            got = shifted(sent, -width).astype(jnp.float32)
            acc = [acc[i] + got[i * tok:(i + 1) * tok] if i < take else acc[i] for i in range(width)]
        total = acc[0]
        key_gradient = total[:, :key_width].astype(jnp.bfloat16)
        value_gradient = total[:, key_width:].astype(jnp.bfloat16)
        grad_q = from_rows(scale * dq, tok).astype(jnp.bfloat16)
        return (grad_q, key_gradient, value_gradient, grad_wo)

    return per_device


def solution(mesh):
    devs = mesh.devices.reshape(2, mesh.shape["ctx"] // 4, 2, mesh.shape["head"])
    sub_mesh = jax.sharding.Mesh(devs, CTX_PARTS + ("head",))
    return jax.shard_map(
        make_per_device(mesh.shape["ctx"]),
        mesh=sub_mesh,
        in_specs=(
            P(CTX_PARTS, "head"),
            P(CTX_PARTS, "head"),
            P(CTX_PARTS, "head"),
            P(CTX_PARTS, "head"),
            P("head", None),
            P(),
        ),
        out_specs=(P(CTX_PARTS, "head"), P(CTX_PARTS, "head"), P(CTX_PARTS, "head"), P(CTX_PARTS, "head")),
        check_vma=False,
    )
```

```python
import jax
import jax.numpy as jnp
from jax import lax
from jax.sharding import PartitionSpec as P

HEAD_SIZE = 128
MOST = 3744
CTX_PARTS = ("ctx_x", "ctx_z", "ctx_core")


def to_rows(x, kv_heads):
    tok = x.shape[0]
    group = x.shape[1] // (kv_heads * HEAD_SIZE)
    x = x.reshape(tok, kv_heads, group, HEAD_SIZE).transpose(1, 2, 0, 3)
    return x.reshape(kv_heads, group * tok, HEAD_SIZE)


def from_rows(x, tok):
    kv_heads, rows, d = x.shape
    group = rows // tok
    x = x.reshape(kv_heads, group, tok, d).transpose(2, 0, 1, 3)
    return x.reshape(tok, kv_heads * group * d)


def make_per_device(n_ctx):
    def per_device(queries, rotated_key_rows, value_matrix, out_grad, w_out, doc_lengths):
        tok = queries.shape[0]
        kv_heads = rotated_key_rows.shape[1] // HEAD_SIZE
        group = queries.shape[1] // (kv_heads * HEAD_SIZE)
        key_width = kv_heads * HEAD_SIZE
        scale = HEAD_SIZE ** (-0.5)
        back = -(-(MOST - 1) // tok)
        n_slots = min(n_ctx, back + 1)

        me = lax.axis_index(CTX_PARTS)
        my_first = me * tok
        my_positions = my_first + jnp.arange(tok, dtype=jnp.int32)
        doc_ends = jnp.cumsum(doc_lengths)
        my_segs = jnp.sum(
            jnp.where(doc_ends[None, :] <= my_positions[:, None], doc_lengths[None, :], 0), axis=1
        ).astype(jnp.int32)
        q_pos = jnp.tile(my_positions, group)
        q_seg = jnp.tile(my_segs, group)

        q_rows = to_rows(queries, kv_heads)
        kv_local = jnp.concatenate([rotated_key_rows, value_matrix], axis=1)

        def shifted(x, shift):
            return lax.ppermute(x, CTX_PARTS, [(i, (i + shift) % n_ctx) for i in range(n_ctx)])

        kv_slots = [kv_local]
        width = 1
        while width < min(n_slots, 4):
            take = min(width, n_slots - width)
            got = shifted(jnp.concatenate(kv_slots[:take], axis=0), width)
            kv_slots += [got[i * tok:(i + 1) * tok] for i in range(take)]
            width *= 2
        base = jnp.concatenate(kv_slots[:width], axis=0)
        for shift in range(width, n_slots, width):
            take = min(width, n_slots - shift)
            got = shifted(base[: take * tok], shift)
            kv_slots += [got[i * tok:(i + 1) * tok] for i in range(take)]

        grad_cols = lax.all_gather(out_grad, "head", axis=1, tiled=True)

        def slot_parts(s):
            kvs = kv_slots[s]
            k_s = kvs[:, :key_width].reshape(tok, kv_heads, HEAD_SIZE).transpose(1, 0, 2)
            v_s = kvs[:, key_width:].reshape(tok, kv_heads, HEAD_SIZE).transpose(1, 0, 2)
            blk = (me - s) % n_ctx
            key_pos = blk * tok + jnp.arange(tok, dtype=jnp.int32)
            allowed = (key_pos[None, :] <= q_pos[:, None]) & (key_pos[None, :] >= q_seg[:, None])
            scores = (
                jnp.einsum("grd,gkd->grk", q_rows, k_s, preferred_element_type=jnp.float32) * scale
            )
            return k_s, v_s, allowed[None], scores

        weighted = jnp.zeros((kv_heads, group * tok, HEAD_SIZE), jnp.float32)
        totals = jnp.zeros((kv_heads, group * tok), jnp.float32)
        for s in range(n_slots):
            k_s, v_s, allowed, scores = slot_parts(s)
            expo = jnp.where(allowed, jnp.exp(scores), 0.0)
            totals = totals + jnp.sum(expo, axis=2)
            weighted = weighted + jnp.einsum(
                "grk,gkd->grd", expo.astype(jnp.bfloat16), v_s, preferred_element_type=jnp.float32
            )
        attn = (weighted / totals[..., None]).astype(jnp.bfloat16)
        log_total = jnp.log(totals)
        attn_flat = from_rows(attn, tok)

        grad_attn = lax.dot_general(
            grad_cols, w_out, (((1,), (1,)), ((), ())), preferred_element_type=jnp.float32
        ).astype(jnp.bfloat16)
        g_rows = to_rows(grad_attn, kv_heads)
        row_delta = jnp.sum(g_rows.astype(jnp.float32) * attn.astype(jnp.float32), axis=2)

        wo_part = lax.dot_general(
            grad_cols, attn_flat, (((0,), (0,)), ((), ())), preferred_element_type=jnp.float32
        ).astype(jnp.bfloat16)
        wo_part, g_rows, row_delta = lax.optimization_barrier((wo_part, g_rows, row_delta))
        wo_rows = wo_part.shape[0] // n_ctx
        sizes = [lax.axis_size(a) for a in CTX_PARTS]
        staged = wo_part.reshape(*sizes, wo_rows, wo_part.shape[1])
        order = (2, 0, 1)
        staged = staged.transpose(*order, 3, 4).reshape(wo_part.shape)
        for a in [CTX_PARTS[i] for i in order]:
            staged = lax.psum_scatter(staged, a, scatter_dimension=0, tiled=True)
        grad_wo = staged

        dq = jnp.zeros((kv_heads, group * tok, HEAD_SIZE), jnp.float32)
        parts = [None] * n_slots
        for s in reversed(range(n_slots)):
            k_s, v_s, allowed, scores = slot_parts(s)
            weights = jnp.where(allowed, jnp.exp(scores - log_total[..., None]), 0.0)
            grad_weights = jnp.einsum(
                "grd,gkd->grk", g_rows, v_s, preferred_element_type=jnp.float32
            )
            dscore = (weights * (grad_weights - row_delta[..., None])).astype(jnp.bfloat16)
            dq = dq + jnp.einsum("grk,gkd->grd", dscore, k_s, preferred_element_type=jnp.float32)
            dk = jnp.einsum("grk,grd->gkd", dscore, q_rows, preferred_element_type=jnp.float32)
            dv = jnp.einsum(
                "grk,grd->gkd", weights.astype(jnp.bfloat16), g_rows,
                preferred_element_type=jnp.float32,
            )
            part = jnp.concatenate(
                [
                    (scale * dk).transpose(1, 0, 2).reshape(tok, key_width),
                    dv.transpose(1, 0, 2).reshape(tok, key_width),
                ],
                axis=1,
            )
            parts[s] = part
        acc = parts[:width]
        for shift in range(width, n_slots, width):
            take = min(width, n_slots - shift)
            sent = jnp.concatenate(parts[shift:shift + take], axis=0).astype(jnp.bfloat16)
            got = shifted(sent, -shift).astype(jnp.float32)
            for i in range(take):
                acc[i] = acc[i] + got[i * tok:(i + 1) * tok]
        while width > 1:
            width //= 2
            take = min(width, len(acc) - width)
            sent = jnp.concatenate(acc[width:width + take], axis=0).astype(jnp.bfloat16)
            got = shifted(sent, -width).astype(jnp.float32)
            acc = [acc[i] + got[i * tok:(i + 1) * tok] if i < take else acc[i] for i in range(width)]
        total = acc[0]
        key_gradient = total[:, :key_width].astype(jnp.bfloat16)
        value_gradient = total[:, key_width:].astype(jnp.bfloat16)
        grad_q = from_rows(scale * dq, tok).astype(jnp.bfloat16)
        return (grad_q, key_gradient, value_gradient, grad_wo)

    return per_device


def solution(mesh):
    devs = mesh.devices.reshape(2, mesh.shape["ctx"] // 4, 2, mesh.shape["head"])
    sub_mesh = jax.sharding.Mesh(devs, CTX_PARTS + ("head",))
    return jax.shard_map(
        make_per_device(mesh.shape["ctx"]),
        mesh=sub_mesh,
        in_specs=(
            P(CTX_PARTS, "head"),
            P(CTX_PARTS, "head"),
            P(CTX_PARTS, "head"),
            P(CTX_PARTS, "head"),
            P("head", None),
            P(),
        ),
        out_specs=(P(CTX_PARTS, "head"), P(CTX_PARTS, "head"), P(CTX_PARTS, "head"), P(CTX_PARTS, "head")),
        check_vma=False,
    )
```

```python
import jax
import jax.numpy as jnp
from jax import lax
from jax.sharding import PartitionSpec as P

HEAD_SIZE = 128
MOST = 3744


def to_rows(x, kv_heads):
    tok = x.shape[0]
    group = x.shape[1] // (kv_heads * HEAD_SIZE)
    x = x.reshape(tok, kv_heads, group, HEAD_SIZE).transpose(1, 2, 0, 3)
    return x.reshape(kv_heads, group * tok, HEAD_SIZE)


def from_rows(x, tok):
    kv_heads, rows, d = x.shape
    group = rows // tok
    x = x.reshape(kv_heads, group, tok, d).transpose(2, 0, 1, 3)
    return x.reshape(tok, kv_heads * group * d)


def make_per_device(n_ctx):
    def per_device(queries, rotated_key_rows, value_matrix, out_grad, w_out, doc_lengths):
        tok = queries.shape[0]
        kv_heads = rotated_key_rows.shape[1] // HEAD_SIZE
        group = queries.shape[1] // (kv_heads * HEAD_SIZE)
        key_width = kv_heads * HEAD_SIZE
        scale = HEAD_SIZE ** (-0.5)
        back = -(-(MOST - 1) // tok)
        n_slots = min(n_ctx, back + 1)

        me = lax.axis_index("ctx")
        my_first = me * tok
        my_positions = my_first + jnp.arange(tok, dtype=jnp.int32)
        doc_ends = jnp.cumsum(doc_lengths)
        my_segs = jnp.sum(
            jnp.where(doc_ends[None, :] <= my_positions[:, None], doc_lengths[None, :], 0), axis=1
        ).astype(jnp.int32)
        q_pos = jnp.tile(my_positions, group)
        q_seg = jnp.tile(my_segs, group)

        q_rows = to_rows(queries, kv_heads)
        kv_local = jnp.concatenate([rotated_key_rows, value_matrix], axis=1)

        def shifted(x, shift):
            return lax.ppermute(x, "ctx", [(i, (i + shift) % n_ctx) for i in range(n_ctx)])

        kv_slots = [kv_local]
        width = 1
        while width < min(n_slots, 4):
            take = min(width, n_slots - width)
            got = shifted(jnp.concatenate(kv_slots[:take], axis=0), width)
            kv_slots += [got[i * tok:(i + 1) * tok] for i in range(take)]
            width *= 2
        base = jnp.concatenate(kv_slots[:width], axis=0)
        for shift in range(width, n_slots, width):
            take = min(width, n_slots - shift)
            got = shifted(base[: take * tok], shift)
            kv_slots += [got[i * tok:(i + 1) * tok] for i in range(take)]

        grad_cols = lax.all_gather(out_grad, "head", axis=1, tiled=True)

        def slot_parts(s):
            kvs = kv_slots[s]
            k_s = kvs[:, :key_width].reshape(tok, kv_heads, HEAD_SIZE).transpose(1, 0, 2)
            v_s = kvs[:, key_width:].reshape(tok, kv_heads, HEAD_SIZE).transpose(1, 0, 2)
            blk = (me - s) % n_ctx
            key_pos = blk * tok + jnp.arange(tok, dtype=jnp.int32)
            allowed = (key_pos[None, :] <= q_pos[:, None]) & (key_pos[None, :] >= q_seg[:, None])
            scores = (
                jnp.einsum("grd,gkd->grk", q_rows, k_s, preferred_element_type=jnp.float32) * scale
            )
            return k_s, v_s, allowed[None], scores

        weighted = jnp.zeros((kv_heads, group * tok, HEAD_SIZE), jnp.float32)
        totals = jnp.zeros((kv_heads, group * tok), jnp.float32)
        for s in range(n_slots):
            k_s, v_s, allowed, scores = slot_parts(s)
            expo = jnp.where(allowed, jnp.exp(scores), 0.0)
            totals = totals + jnp.sum(expo, axis=2)
            weighted = weighted + jnp.einsum(
                "grk,gkd->grd", expo.astype(jnp.bfloat16), v_s,
                preferred_element_type=jnp.float32,
            )
        attn = (weighted / totals[..., None]).astype(jnp.bfloat16)
        log_total = jnp.log(totals)
        attn_flat = from_rows(attn, tok)

        grad_attn = lax.dot_general(
            grad_cols, w_out, (((1,), (1,)), ((), ())), preferred_element_type=jnp.float32
        ).astype(jnp.bfloat16)
        g_rows = to_rows(grad_attn, kv_heads)
        row_delta = jnp.sum(g_rows.astype(jnp.float32) * attn.astype(jnp.float32), axis=2)

        wo_part = lax.dot_general(
            grad_cols, attn_flat, (((0,), (0,)), ((), ())), preferred_element_type=jnp.float32
        ).astype(jnp.bfloat16)
        wo_part, g_rows, row_delta = lax.optimization_barrier((wo_part, g_rows, row_delta))
        grad_wo = lax.psum_scatter(wo_part, "ctx", scatter_dimension=0, tiled=True)

        dq = jnp.zeros((kv_heads, group * tok, HEAD_SIZE), jnp.float32)
        parts = [None] * n_slots
        for s in reversed(range(n_slots)):
            k_s, v_s, allowed, scores = slot_parts(s)
            weights = jnp.where(allowed, jnp.exp(scores - log_total[..., None]), 0.0)
            grad_weights = jnp.einsum(
                "grd,gkd->grk", g_rows, v_s, preferred_element_type=jnp.float32
            )
            dscore = (weights * (grad_weights - row_delta[..., None])).astype(jnp.bfloat16)
            dq = dq + jnp.einsum("grk,gkd->grd", dscore, k_s, preferred_element_type=jnp.float32)
            dk = jnp.einsum("grk,grd->gkd", dscore, q_rows, preferred_element_type=jnp.float32)
            dv = jnp.einsum(
                "grk,grd->gkd", weights.astype(jnp.bfloat16), g_rows,
                preferred_element_type=jnp.float32,
            )
            part = jnp.concatenate(
                [
                    (scale * dk).transpose(1, 0, 2).reshape(tok, key_width),
                    dv.transpose(1, 0, 2).reshape(tok, key_width),
                ],
                axis=1,
            )
            parts[s] = part
        acc = parts[:width]
        for shift in range(width, n_slots, width):
            take = min(width, n_slots - shift)
            sent = jnp.concatenate(parts[shift:shift + take], axis=0).astype(jnp.bfloat16)
            got = shifted(sent, -shift).astype(jnp.float32)
            for i in range(take):
                acc[i] = acc[i] + got[i * tok:(i + 1) * tok]
        while width > 1:
            width //= 2
            take = min(width, len(acc) - width)
            sent = jnp.concatenate(acc[width:width + take], axis=0).astype(jnp.bfloat16)
            got = shifted(sent, -width).astype(jnp.float32)
            acc = [acc[i] + got[i * tok:(i + 1) * tok] if i < take else acc[i] for i in range(width)]
        total = acc[0]
        key_gradient = total[:, :key_width].astype(jnp.bfloat16)
        value_gradient = total[:, key_width:].astype(jnp.bfloat16)
        grad_q = from_rows(scale * dq, tok).astype(jnp.bfloat16)
        return (grad_q, key_gradient, value_gradient, grad_wo)

    return per_device


def solution(mesh):
    def body(*args):
        return make_per_device(mesh.shape["ctx"])(*args)

    return step_of(mesh, body)


def step_of(mesh, body):
    return jax.shard_map(
        body,
        mesh=mesh,
        in_specs=(
            P("ctx", "head"),
            P("ctx", "head"),
            P("ctx", "head"),
            P("ctx", "head"),
            P("head", None),
            P(),
        ),
        out_specs=(P("ctx", "head"), P("ctx", "head"), P("ctx", "head"), P("ctx", "head")),
        check_vma=False,
    )
```
